32 devices in a mesh: row: 8 (over y, x, core), col: 4 (over z).
Axes of the slice: x: 2, y: 2, z: 4, core: 2. Of those that a mesh axis runs over, the one named last changes fastest.
Arguments:
- tensor: float32 [128, 128, 768], P('row', 'col'), may hold values from -6 to 6
- start_one: float32 [128, 64], P('row'), may hold values from -0.5 to 0.5
- start_two: float32 [128, 64], P('col'), may hold values from -0.5 to 0.5
- start_three: float32 [768, 64], replicated, may hold values from -0.21875 to 0.21875
Outputs:
- factor_one: float32 [128, 64], replicated
- factor_two: float32 [128, 64], replicated
- factor_three: float32 [768, 64], replicated
- core: float32 [64, 64, 64], P(None, 'row', 'col')
The draws below stay inside these ranges and needn't reach their ends.
All inputs are finite; a program needn't handle non-finite values.
Results may differ from the reference program's by a relative error of at most 0.0003.
Values sent between devices are 32-bit elements; how exact they have to be, the bound alone decides.
A program may use at most 64 MiB of HBM per device.

```python
import math
import jax
import jax.numpy as jnp
from jax import lax

N3 = 768
RANK = 64
STEPS = 4
N1 = 128
N2 = 128


def levels(key, extent, cuts, least, top_value):
    def one(position, parts):
        steps = jax.random.uniform(jax.random.fold_in(jax.random.fold_in(key, 6), position), (parts,), jnp.float32, least / len(cuts), top_value / len(cuts))
        return jnp.repeat(jnp.exp(steps), extent[position] // parts).reshape((-1,) + (1,) * (len(extent) - position - 1))

    gain = one(*cuts[0])
    for cut in cuts[1:]:
        gain = gain * one(*cut)
    return gain


def centred(own_key, extent, scale, reach, shards=(), held_as=jnp.bfloat16):
    gain = levels(own_key, extent, shards, -0.22, 0.18) if shards else 1.0
    array = jax.random.normal(own_key, extent, jnp.float32) * scale * gain
    return jnp.minimum(jnp.maximum(array, -reach), reach).astype(held_as)


def setup_inputs(seed: int = 0) -> dict:
    seeds = jax.random.split(jax.random.key(seed), 5)
    return {
        "tensor": centred(seeds[0], (N1, N2, N3), 1.0, 6.0, ((0, 8), (1, 4)), jnp.float32),
        "start_one": centred(seeds[1], (N1, RANK), N1 ** -0.5, 0.5, ((0, 8),), jnp.float32),
        "start_two": centred(seeds[2], (N2, RANK), N2 ** -0.5, 0.5, ((0, 4),), jnp.float32),
        "start_three": centred(seeds[3], (N3, RANK), N3 ** -0.5, 0.21875, (), jnp.float32),
    }


HIGHEST = lax.Precision.HIGHEST

def orthonormal(matrix):
    inner = jnp.dot(matrix.T.astype(jnp.float32), matrix.astype(jnp.float32), precision=HIGHEST, preferred_element_type=jnp.float32)
    lower = jnp.linalg.cholesky(inner)
    return jax.scipy.linalg.solve_triangular(lower, matrix.T, lower=True).T

def iterate(gram, start):
    basis = start
    for iteration in range(STEPS):
        basis = orthonormal(jnp.dot(gram.astype(jnp.float32), basis.astype(jnp.float32), precision=HIGHEST, preferred_element_type=jnp.float32))
    return basis

def self_gram(slab):
    return jnp.dot(slab.astype(jnp.float32), slab.T.astype(jnp.float32), precision=HIGHEST, preferred_element_type=jnp.float32)

def reference(tensor, start_one, start_two, start_three):
    contracted = jnp.einsum('ijk,kc->ijc', tensor, start_three, precision=HIGHEST)
    slab_one = jnp.einsum('ijc,jb->ibc', contracted, start_two, precision=HIGHEST).reshape(N1, RANK * RANK)
    basis_one = iterate(self_gram(slab_one), start_one)
    slab_two = jnp.einsum('ijc,ia->jac', contracted, basis_one, precision=HIGHEST).reshape(N2, RANK * RANK)
    basis_two = iterate(self_gram(slab_two), start_two)
    partial_three = jnp.einsum('ijk,ia->ajk', tensor, basis_one, precision=HIGHEST)
    slab_three = jnp.einsum('ajk,jb->kab', partial_three, basis_two, precision=HIGHEST).reshape(N3, RANK * RANK)
    basis_three = iterate(self_gram(slab_three), start_three)
    core = jnp.dot(basis_three.T.astype(jnp.float32), slab_three.astype(jnp.float32), precision=HIGHEST, preferred_element_type=jnp.float32).reshape(RANK, RANK, RANK)
    factor_one = basis_one * math.sqrt(N1)
    factor_two = basis_two * math.sqrt(N2)
    factor_three = basis_three * math.sqrt(N3)
    return (factor_one, factor_two, factor_three, core)
```

```python
import functools
import math

import jax
import jax.numpy as jnp
from jax import lax
from jax.experimental import pallas as pl
from jax.experimental.pallas import tpu as pltpu
from jax.sharding import PartitionSpec as P

STEPS = 4


HIGHEST = lax.Precision.HIGHEST
MESH = pl.DeviceIdType.MESH
SUBLANES = 8
BLOCK = 8


def product(left, right):
    return jnp.dot(left, right, precision=HIGHEST, preferred_element_type=jnp.float32)


def left_product(left, right):
    return lax.dot_general(
        left, right, (((0,), (0,)), ((), ())), precision=HIGHEST, preferred_element_type=jnp.float32
    )


def right_product(left, right):
    return lax.dot_general(
        left, right, (((1,), (1,)), ((), ())), precision=HIGHEST, preferred_element_type=jnp.float32
    )


def cross_product(left, right):
    return lax.dot_general(
        left, right, (((0,), (1,)), ((), ())), precision=HIGHEST, preferred_element_type=jnp.float32
    )


def orthonormal(matrix, inner):
    lower = jnp.linalg.cholesky(inner)
    return jax.scipy.linalg.solve_triangular(lower, matrix.T, lower=True).T


def settle(gram_whole, basis):
    for iteration in range(STEPS):
        image = product(gram_whole, basis)
        basis = orthonormal(image, left_product(image, image))
    return basis


def general(tensor, start_one, start_two, start_three):
    rows_one, rows_two, depth = tensor.shape
    rank = start_three.shape[1]
    flat = tensor.reshape(rows_one * rows_two, depth)
    contracted = cross_product(start_three, flat).reshape(rank, rows_one, rows_two)
    part_one = jnp.einsum("cij,jb->ibc", contracted, start_two, precision=HIGHEST).reshape(
        rows_one, rank * rank
    )
    slab_one = lax.psum_scatter(part_one, "col", scatter_dimension=1, tiled=True)
    slab_rows_one = lax.all_gather(slab_one, "row", axis=0, tiled=True)
    gram_one = lax.psum(right_product(slab_rows_one, slab_rows_one), "col")
    basis_one = settle(gram_one, lax.all_gather(start_one, "row", axis=0, tiled=True))
    own_one = lax.dynamic_slice_in_dim(basis_one, lax.axis_index("row") * rows_one, rows_one, 0)
    part_two = jnp.einsum("cij,ia->jac", contracted, own_one, precision=HIGHEST).reshape(
        rows_two, rank * rank
    )
    slab_two = lax.psum_scatter(part_two, "row", scatter_dimension=1, tiled=True)
    slab_rows_two = lax.all_gather(slab_two, "col", axis=0, tiled=True)
    gram_two = lax.psum(right_product(slab_rows_two, slab_rows_two), "row")
    basis_two = settle(gram_two, lax.all_gather(start_two, "col", axis=0, tiled=True))
    own_two = lax.dynamic_slice_in_dim(basis_two, lax.axis_index("col") * rows_two, rows_two, 0)
    received = lax.all_to_all(tensor, "row", split_axis=2, concat_axis=0, tiled=True)
    count, items, cells = received.shape
    merged = left_product(basis_one, received.reshape(count, items * cells))
    mixed = merged.reshape(rank, items, cells)
    part_three = jnp.einsum("ajk,jb->kba", mixed, own_two, precision=HIGHEST)
    cells_here = part_three.shape[0]
    slab_three = lax.psum_scatter(
        part_three.reshape(cells_here, rank * rank), "col", scatter_dimension=1, tiled=True
    )
    gram_part_three = right_product(slab_three, lax.all_gather(slab_three, "row", axis=0, tiled=True))
    gram_three = lax.psum(gram_part_three, "col")
    basis_three = start_three
    own_three = start_three
    for iteration in range(STEPS):
        image = product(gram_three, basis_three)
        inner = lax.psum(left_product(image, image), "row")
        own_three = orthonormal(image, inner)
        basis_three = lax.all_gather(own_three, "row", axis=0, tiled=True)
    core_part = left_product(own_three, slab_three)
    core_part = core_part.reshape(rank, core_part.shape[1] // rank, rank)
    core = lax.psum_scatter(core_part, "row", scatter_dimension=2, tiled=True).transpose(0, 2, 1)
    factor_one = basis_one * math.sqrt(basis_one.shape[0])
    factor_two = basis_two * math.sqrt(basis_two.shape[0])
    factor_three = basis_three * math.sqrt(basis_three.shape[0])
    return (factor_one, factor_two, factor_three, core)


def inverse_factor(inner):
    n = inner.shape[0]
    groups = n // SUBLANES
    eye = (
        lax.broadcasted_iota(jnp.int32, (n, n), 0) == lax.broadcasted_iota(jnp.int32, (n, n), 1)
    ).astype(jnp.float32)
    whole = jnp.concatenate([inner, eye], axis=1)
    width = whole.shape[1]
    rows = [whole[g * SUBLANES : (g + 1) * SUBLANES] for g in range(groups)]
    sub = lax.broadcasted_iota(jnp.int32, (SUBLANES, width), 0)
    pivots = [None] * n
    shape = (SUBLANES, width)
    for base in range(groups):
        columns = [
            [jnp.broadcast_to(rows[g][:, k : k + 1], shape) for g in range(base, groups)]
            for k in range(base * SUBLANES, (base + 1) * SUBLANES)
        ]
        for t in range(SUBLANES):
            pivot = jnp.broadcast_to(columns[t][0][t : t + 1, :], shape)
            scale = 1.0 / pivot
            pivots[base * SUBLANES + t] = pivot
            row = jnp.broadcast_to(rows[base][t : t + 1, :], shape)
            heads = [
                jnp.broadcast_to(columns[s][0][t : t + 1, :], shape) for s in range(t + 1, SUBLANES)
            ]
            for g in range(base, groups):
                factor = columns[t][g - base] * scale
                if g == base:
                    factor = jnp.where(sub > t, factor, 0.0)
                rows[g] = rows[g] - factor * row
                for s in range(t + 1, SUBLANES):
                    columns[s][g - base] = columns[s][g - base] - factor * heads[s - t - 1]
    out = []
    for g in range(groups):
        held = pivots[g * SUBLANES]
        for t in range(1, SUBLANES):
            held = jnp.where(sub == t, pivots[g * SUBLANES + t], held)
        out.append(rows[g] * lax.rsqrt(held))
    return jnp.concatenate(out, axis=0)[:, n:]


def orth(image):
    return right_product(image, inverse_factor(left_product(image, image)))


def steps_on(gram_ref, start_ref, basis_ref):
    basis_ref[...] = start_ref[...]

    def one(_, carry):
        basis_ref[...] = orth(product(gram_ref[...], basis_ref[...]))
        return carry

    lax.fori_loop(0, STEPS, one, 0)


def gram_one_kernel(held_ref, start_ref, gram_ref):
    slabs = [product(held_ref[c], start_ref[...]) for c in range(held_ref.shape[0])]
    total = right_product(slabs[0], slabs[0])
    for slab in slabs[1:]:
        total = total + right_product(slab, slab)
    gram_ref[...] = total


def mode_one_kernel(gram_ref, start_ref, held_ref, basis_ref, next_ref):
    steps_on(gram_ref, start_ref, basis_ref)
    basis = basis_ref[...]
    total = None
    for c in range(held_ref.shape[0]):
        slab = left_product(held_ref[c], basis)
        term = right_product(slab, slab)
        total = term if total is None else total + term
    next_ref[...] = total


def mode_two_kernel(gram_ref, start_ref, one_ref, cube_ref, basis_ref, slab_ref):
    steps_on(gram_ref, start_ref, basis_ref)
    basis = basis_ref[...]
    one = one_ref[...]
    cells, rank, _ = slab_ref.shape
    count = one_ref.shape[0]
    for k in range(cells):
        face = cube_ref[pl.ds(k, count, stride=cells), :]
        slab_ref[k] = product(left_product(one, face), basis)


def pack(image):
    half = image.shape[0] // 2
    return jnp.concatenate([image[:half], image[half:]], axis=1)


def unpack(packed):
    half = packed.shape[1] // 2
    return jnp.concatenate([packed[:, :half], packed[:, half:]], axis=0)


def apply_gram(slab, basis):
    return pack(product(slab, left_product(slab, basis)))


def first_image_kernel(slab_ref, basis_ref, image_ref):
    image_ref[...] = apply_gram(slab_ref[...], basis_ref[...])


def image_kernel(packed_ref, slab_ref, image_ref):
    image_ref[...] = apply_gram(slab_ref[...], orth(unpack(packed_ref[...])))


def last_kernel(packed_ref, slab_ref, factor_ref, core_ref):
    basis = orth(unpack(packed_ref[...]))
    factor_ref[...] = basis * math.sqrt(basis.shape[0])
    core_ref[...] = left_product(basis, slab_ref[...])


def on_core(kernel, shapes, *operands):
    outs = [jax.ShapeDtypeStruct(shape, jnp.float32) for shape in shapes]
    spec = pl.BlockSpec(memory_space=pltpu.VMEM)
    cost = pl.CostEstimate(flops=2 * 10**9, bytes_accessed=2 * 10**6, transcendentals=0)
    return pl.pallas_call(
        kernel,
        out_shape=outs,
        in_specs=[spec] * len(operands),
        out_specs=[spec] * len(outs),
        cost_estimate=cost,
    )(*operands)


def sum_kernel(n_row, n_col, x_ref, o_ref, parts, planes, s1, r1, s2, r2, s3, r3):
    row, col = lax.axis_index("row"), lax.axis_index("col")
    count = x_ref.shape[0] // n_row

    def mine(which):
        return pl.ds(pl.multiple_of(which * count, SUBLANES), count)

    def row_peer(d):
        return (lax.rem(row + d, n_row), col)

    def col_peer(d):
        return (row, lax.rem(col + d, n_col))

    barrier = pltpu.get_barrier_semaphore()
    for d in range(1, n_row):
        pl.semaphore_signal(barrier, inc=1, device_id=row_peer(d), device_id_type=MESH)
    for d in range(1, n_col):
        pl.semaphore_signal(barrier, inc=1, device_id=col_peer(d), device_id_type=MESH)
    pl.semaphore_wait(barrier, n_row + n_col - 2)

    def copies(n, peer, source, target, send, recv):
        made = [
            pltpu.make_async_remote_copy(
                src_ref=source(d),
                dst_ref=target(d),
                send_sem=send.at[d],
                recv_sem=recv.at[d],
                device_id=peer(d),
                device_id_type=MESH,
            )
            for d in range(1, n)
        ]
        for copy in made:
            copy.start()
        return made

    first = copies(n_row, row_peer, lambda d: x_ref.at[mine(row_peer(d)[0])], lambda d: parts.at[d], s1, r1)
    total = x_ref[mine(row), :]
    for d in range(1, n_row):
        first[d - 1].wait_recv()
        total = total + parts[d]
    planes[col] = total
    second = copies(n_col, col_peer, lambda d: planes.at[col], lambda d: planes.at[col], s2, r2)
    for copy in second:
        copy.wait_recv()
    total = planes[0]
    for q in range(1, n_col):
        total = total + planes[q]
    o_ref[mine(row), :] = total
    third = copies(n_row, row_peer, lambda d: o_ref.at[mine(row)], lambda d: o_ref.at[mine(row)], s3, r3)
    for copy in third:
        copy.wait_recv()
    for copy in first + second + third:
        copy.wait_send()


def sum_all(n_row, n_col, name, collective_id, x):
    spec = pl.BlockSpec(memory_space=pltpu.VMEM)
    count = x.shape[0] // n_row
    dma = pltpu.SemaphoreType.DMA
    return pl.pallas_call(
        functools.partial(sum_kernel, n_row, n_col),
        out_shape=jax.ShapeDtypeStruct(x.shape, x.dtype),
        in_specs=[spec],
        out_specs=spec,
        scratch_shapes=[
            pltpu.VMEM((n_row, count, x.shape[1]), x.dtype),
            pltpu.VMEM((n_col, count, x.shape[1]), x.dtype),
            dma((n_row,)),
            dma((n_row,)),
            dma((n_col,)),
            dma((n_col,)),
            dma((n_row,)),
            dma((n_row,)),
        ],
        compiler_params=pltpu.CompilerParams(collective_id=collective_id, has_side_effects=True),
        cost_estimate=pl.CostEstimate(flops=10**9, bytes_accessed=10**7, transcendentals=0),
        name=name,
    )(x)


def shared(n_row, n_col, tensor, start_one, start_two, start_three):
    rows_one, rows_two, depth = tensor.shape
    rank = start_three.shape[1]
    both = ("row", "col")
    n = n_row * n_col
    n_one, n_two = rows_one * n_row, rows_two * n_col

    whole_one = lax.all_gather(start_one, "row", axis=0, tiled=True)
    whole_two = lax.all_gather(start_two, "col", axis=0, tiled=True)

    flat = tensor.reshape(rows_one * rows_two, depth)
    contracted = cross_product(start_three, flat).reshape(n, rank // n, rows_one, rows_two)
    held = lax.all_to_all(contracted, both, split_axis=0, concat_axis=0, tiled=True)
    held = held.reshape(n_row, n_col, rank // n, rows_one, rows_two).transpose(2, 0, 3, 1, 4)
    held = held.reshape(rank // n, n_one, n_two)

    strips = lax.all_to_all(tensor, "col", split_axis=0, concat_axis=1, tiled=True)
    strips = strips.transpose(0, 2, 1)
    cube = lax.all_to_all(strips, both, split_axis=1, concat_axis=0, tiled=True)
    cells = depth // n
    cube = cube.reshape(n_one * cells, n_two)

    add = functools.partial(sum_all, n_row, n_col)
    (part,) = on_core(gram_one_kernel, [(n_one, n_one)], held, whole_two)
    gram_one = add("sum_gram", 1, part)
    basis_one, part = on_core(
        mode_one_kernel, [(n_one, rank), (n_two, n_two)], gram_one, whole_one, held
    )
    gram_two = add("sum_gram", 1, part)
    basis_two, slab = on_core(
        mode_two_kernel,
        [(n_two, rank), (cells, rank, rank)],
        gram_two,
        whole_two,
        basis_one,
        cube,
    )
    own_a, own_b = rank // n_row, rank // n_col
    slab = slab.reshape(cells, n_row, own_a, n_col, own_b).transpose(1, 3, 0, 2, 4)
    slab = slab.reshape(n, cells, own_a * own_b)
    slab = lax.all_to_all(slab, both, split_axis=0, concat_axis=0, tiled=True)
    slab = slab.reshape(depth, own_a * own_b)

    packed_shape = (depth // 2, 2 * rank)
    (part,) = on_core(first_image_kernel, [packed_shape], slab, start_three)
    for iteration in range(STEPS - 1):
        (part,) = on_core(image_kernel, [packed_shape], add("sum_image", 2, part), slab)
    factor_three, core = on_core(
        last_kernel,
        [(depth, rank), (rank, own_a * own_b)],
        add("sum_image", 2, part),
        slab,
    )
    factor_one = basis_one * math.sqrt(n_one)
    factor_two = basis_two * math.sqrt(n_two)
    return (factor_one, factor_two, factor_three, core.reshape(rank, own_a, own_b))


def solution(mesh):
    n_row, n_col = mesh.shape["row"], mesh.shape["col"]
    n = n_row * n_col

    def on_device(tensor, start_one, start_two, start_three):
        rows_one, rows_two, depth = tensor.shape
        rank = start_three.shape[1]
        even = (
            rank % n == 0
            and depth % (2 * n_row * SUBLANES) == 0
            and depth % (n * SUBLANES) == 0
            and rows_one % SUBLANES == 0
            and rows_one * n_row == rows_two * n_col
            and rows_one % n_col == 0
        )
        if even:
            return shared(n_row, n_col, tensor, start_one, start_two, start_three)
        return general(tensor, start_one, start_two, start_three)

    return jax.shard_map(
        on_device,
        mesh=mesh,
        in_specs=(P("row", "col", None), P("row", None), P("col", None), P()),
        out_specs=(P(), P(), P(), P(None, "row", "col")),
        check_vma=False,
    )
```

```python
import functools
import math

import jax
import jax.numpy as jnp
from jax import lax
from jax.experimental import pallas as pl
from jax.experimental.pallas import tpu as pltpu
from jax.sharding import PartitionSpec as P

STEPS = 4


HIGHEST = lax.Precision.HIGHEST
MESH = pl.DeviceIdType.MESH
SUBLANES = 8
LANES = 128


def product(left, right):
    return jnp.dot(left, right, precision=HIGHEST, preferred_element_type=jnp.float32)


def left_product(left, right):
    return lax.dot_general(
        left, right, (((0,), (0,)), ((), ())), precision=HIGHEST, preferred_element_type=jnp.float32
    )


def right_product(left, right):
    return lax.dot_general(
        left, right, (((1,), (1,)), ((), ())), precision=HIGHEST, preferred_element_type=jnp.float32
    )


def cross_product(left, right):
    return lax.dot_general(
        left, right, (((0,), (1,)), ((), ())), precision=HIGHEST, preferred_element_type=jnp.float32
    )


def orthonormal(matrix, inner):
    lower = jnp.linalg.cholesky(inner)
    return jax.scipy.linalg.solve_triangular(lower, matrix.T, lower=True).T


def settle(gram_whole, basis):
    for iteration in range(STEPS):
        image = product(gram_whole, basis)
        basis = orthonormal(image, left_product(image, image))
    return basis


def general(tensor, start_one, start_two, start_three):
    rows_one, rows_two, depth = tensor.shape
    rank = start_three.shape[1]
    flat = tensor.reshape(rows_one * rows_two, depth)
    contracted = cross_product(start_three, flat).reshape(rank, rows_one, rows_two)
    part_one = jnp.einsum("cij,jb->ibc", contracted, start_two, precision=HIGHEST).reshape(
        rows_one, rank * rank
    )
    slab_one = lax.psum_scatter(part_one, "col", scatter_dimension=1, tiled=True)
    slab_rows_one = lax.all_gather(slab_one, "row", axis=0, tiled=True)
    gram_one = lax.psum(right_product(slab_rows_one, slab_rows_one), "col")
    basis_one = settle(gram_one, lax.all_gather(start_one, "row", axis=0, tiled=True))
    own_one = lax.dynamic_slice_in_dim(basis_one, lax.axis_index("row") * rows_one, rows_one, 0)
    part_two = jnp.einsum("cij,ia->jac", contracted, own_one, precision=HIGHEST).reshape(
        rows_two, rank * rank
    )
    slab_two = lax.psum_scatter(part_two, "row", scatter_dimension=1, tiled=True)
    slab_rows_two = lax.all_gather(slab_two, "col", axis=0, tiled=True)
    gram_two = lax.psum(right_product(slab_rows_two, slab_rows_two), "row")
    basis_two = settle(gram_two, lax.all_gather(start_two, "col", axis=0, tiled=True))
    own_two = lax.dynamic_slice_in_dim(basis_two, lax.axis_index("col") * rows_two, rows_two, 0)
    received = lax.all_to_all(tensor, "row", split_axis=2, concat_axis=0, tiled=True)
    count, items, cells = received.shape
    merged = left_product(basis_one, received.reshape(count, items * cells))
    mixed = merged.reshape(rank, items, cells)
    part_three = jnp.einsum("ajk,jb->kba", mixed, own_two, precision=HIGHEST)
    cells_here = part_three.shape[0]
    slab_three = lax.psum_scatter(
        part_three.reshape(cells_here, rank * rank), "col", scatter_dimension=1, tiled=True
    )
    gram_part_three = right_product(slab_three, lax.all_gather(slab_three, "row", axis=0, tiled=True))
    gram_three = lax.psum(gram_part_three, "col")
    basis_three = start_three
    own_three = start_three
    for iteration in range(STEPS):
        image = product(gram_three, basis_three)
        inner = lax.psum(left_product(image, image), "row")
        own_three = orthonormal(image, inner)
        basis_three = lax.all_gather(own_three, "row", axis=0, tiled=True)
    core_part = left_product(own_three, slab_three)
    core_part = core_part.reshape(rank, core_part.shape[1] // rank, rank)
    core = lax.psum_scatter(core_part, "row", scatter_dimension=2, tiled=True).transpose(0, 2, 1)
    factor_one = basis_one * math.sqrt(basis_one.shape[0])
    factor_two = basis_two * math.sqrt(basis_two.shape[0])
    factor_three = basis_three * math.sqrt(basis_three.shape[0])
    return (factor_one, factor_two, factor_three, core)


def inverse_factor(inner):
    n = inner.shape[0]
    groups = n // SUBLANES
    eye = (
        lax.broadcasted_iota(jnp.int32, (n, n), 0) == lax.broadcasted_iota(jnp.int32, (n, n), 1)
    ).astype(jnp.float32)
    whole = jnp.concatenate([inner, eye], axis=1)
    width = whole.shape[1]
    rows = [whole[g * SUBLANES : (g + 1) * SUBLANES] for g in range(groups)]
    sub = lax.broadcasted_iota(jnp.int32, (SUBLANES, width), 0)
    pivots = [None] * n
    shape = (SUBLANES, width)
    for base in range(groups):
        columns = [
            [jnp.broadcast_to(rows[g][:, k : k + 1], shape) for g in range(base, groups)]
            for k in range(base * SUBLANES, (base + 1) * SUBLANES)
        ]
        for t in range(SUBLANES):
            pivot = jnp.broadcast_to(columns[t][0][t : t + 1, :], shape)
            scale = 1.0 / pivot
            pivots[base * SUBLANES + t] = pivot
            row = jnp.broadcast_to(rows[base][t : t + 1, :], shape)
            heads = [
                jnp.broadcast_to(columns[s][0][t : t + 1, :], shape) for s in range(t + 1, SUBLANES)
            ]
            for g in range(base, groups):
                factor = columns[t][g - base] * scale
                if g == base:
                    factor = jnp.where(sub > t, factor, 0.0)
                rows[g] = rows[g] - factor * row
                for s in range(t + 1, SUBLANES):
                    columns[s][g - base] = columns[s][g - base] - factor * heads[s - t - 1]
    out = []
    for g in range(groups):
        held = pivots[g * SUBLANES]
        for t in range(1, SUBLANES):
            held = jnp.where(sub == t, pivots[g * SUBLANES + t], held)
        out.append(rows[g] * lax.rsqrt(held))
    return jnp.concatenate(out, axis=0)[:, n:]


def orth(image):
    return right_product(image, inverse_factor(left_product(image, image)))


def steps_on(gram_ref, start_ref, basis_ref):
    basis_ref[...] = start_ref[...]

    def one(_, carry):
        basis_ref[...] = orth(product(gram_ref[...], basis_ref[...]))
        return carry

    lax.fori_loop(0, STEPS, one, 0)


def gram_one_kernel(held_ref, start_ref, gram_ref):
    slabs = [product(held_ref[c], start_ref[...]) for c in range(held_ref.shape[0])]
    total = right_product(slabs[0], slabs[0])
    for slab in slabs[1:]:
        total = total + right_product(slab, slab)
    gram_ref[...] = total


def mode_one_kernel(gram_ref, start_ref, held_ref, basis_ref, next_ref):
    steps_on(gram_ref, start_ref, basis_ref)
    basis = basis_ref[...]
    total = None
    for c in range(held_ref.shape[0]):
        slab = left_product(held_ref[c], basis)
        term = right_product(slab, slab)
        total = term if total is None else total + term
    next_ref[...] = total


def lane_groups(width):
    return lax.div(lax.broadcasted_iota(jnp.int32, (1, LANES), 1), width)


def shifted(value, amount):
    amount = amount % LANES
    return value if amount == 0 else pltpu.roll(value, amount, 1)


def mode_two_kernel(n_row, n_col, gram_ref, start_ref, one_ref, cube_ref, basis_ref, send_ref, cube, mixed):
    n, cells, span = cube_ref.shape
    width = LANES // n_col
    rows_one = span // width
    group = lane_groups(width)
    for row in range(n_row):
        for tile in range(span // LANES):
            blocks = [cube_ref[row * n_col + q, :, tile * LANES : (tile + 1) * LANES] for q in range(n_col)]
            for s in range(n_col):
                held = blocks[0]
                held = shifted(held, -s * width)
                for q in range(1, n_col):
                    held = jnp.where(group == q, shifted(blocks[q], (q - s) * width), held)
                item = row * rows_one + tile * n_col + s
                cube[item * cells : (item + 1) * cells, :] = held
    count, rank = one_ref.shape
    one = one_ref[...]
    for k in range(cells):
        face = cube[pl.ds(k, count, stride=cells), :]
        mixed[k * rank : (k + 1) * rank, :] = left_product(one, face)
    steps_on(gram_ref, start_ref, basis_ref)
    basis = basis_ref[...]
    wide = jnp.concatenate([basis, jnp.zeros((basis.shape[0], LANES - rank), jnp.float32)], axis=1)
    own_a, own_b = rank // n_row, rank // n_col
    group = lane_groups(own_b)
    for row in range(n_row):
        rows = [mixed[pl.ds(row * own_a + s, cells, stride=rank), :] for s in range(own_a)]
        slabs = product(jnp.concatenate(rows, axis=0), wide)
        for q in range(n_col):
            held = None
            for s in range(own_a):
                moved = shifted(slabs[s * cells : (s + 1) * cells], (s - q) * own_b)
                held = moved if held is None else jnp.where(group == s, moved, held)
            send_ref[row * n_col + q] = held


def pack(image):
    half = image.shape[0] // 2
    return jnp.concatenate([image[:half], image[half:]], axis=1)


def unpack(packed):
    half = packed.shape[1] // 2
    return jnp.concatenate([packed[:, :half], packed[:, half:]], axis=0)


def apply_gram(slab, basis):
    return pack(product(slab, left_product(slab, basis)))


def image_kernel(packed_ref, slab_ref, image_ref):
    image_ref[...] = apply_gram(slab_ref[...], orth(unpack(packed_ref[...])))


def last_kernel(packed_ref, slab_ref, factor_ref, core_ref):
    basis = orth(unpack(packed_ref[...]))
    factor_ref[...] = basis * math.sqrt(basis.shape[0])
    core_ref[...] = left_product(basis, slab_ref[...])


def on_core(kernel, shapes, *operands, scratch=()):
    outs = [jax.ShapeDtypeStruct(shape, jnp.float32) for shape in shapes]
    spec = pl.BlockSpec(memory_space=pltpu.VMEM)
    cost = pl.CostEstimate(flops=2 * 10**9, bytes_accessed=2 * 10**6, transcendentals=0)
    return pl.pallas_call(
        kernel,
        out_shape=outs,
        in_specs=[spec] * len(operands),
        out_specs=[spec] * len(outs),
        scratch_shapes=[pltpu.VMEM(shape, jnp.float32) for shape in scratch],
        cost_estimate=cost,
    )(*operands)


def sum_kernel(n_row, n_col, x_ref, o_ref, parts, planes, s1, r1, s2, r2, s3, r3):
    row, col = lax.axis_index("row"), lax.axis_index("col")
    count = x_ref.shape[0] // n_row

    def mine(which):
        return pl.ds(pl.multiple_of(which * count, SUBLANES), count)

    def row_peer(d):
        return (lax.rem(row + d, n_row), col)

    def col_peer(d):
        return (row, lax.rem(col + d, n_col))

    barrier = pltpu.get_barrier_semaphore()
    for d in range(1, n_row):
        pl.semaphore_signal(barrier, inc=1, device_id=row_peer(d), device_id_type=MESH)
    for d in range(1, n_col):
        pl.semaphore_signal(barrier, inc=1, device_id=col_peer(d), device_id_type=MESH)
    pl.semaphore_wait(barrier, n_row + n_col - 2)

    def copies(n, peer, source, target, send, recv):
        made = [
            pltpu.make_async_remote_copy(
                src_ref=source(d),
                dst_ref=target(d),
                send_sem=send.at[d],
                recv_sem=recv.at[d],
                device_id=peer(d),
                device_id_type=MESH,
            )
            for d in range(1, n)
        ]
        for copy in made:
            copy.start()
        return made

    first = copies(n_row, row_peer, lambda d: x_ref.at[mine(row_peer(d)[0])], lambda d: parts.at[d], s1, r1)
    total = x_ref[mine(row), :]
    for d in range(1, n_row):
        first[d - 1].wait_recv()
        total = total + parts[d]
    planes[col] = total
    second = copies(n_col, col_peer, lambda d: planes.at[col], lambda d: planes.at[col], s2, r2)
    for copy in second:
        copy.wait_recv()
    total = planes[0]
    for q in range(1, n_col):
        total = total + planes[q]
    o_ref[mine(row), :] = total
    third = copies(n_row, row_peer, lambda d: o_ref.at[mine(row)], lambda d: o_ref.at[mine(row)], s3, r3)
    for copy in third:
        copy.wait_recv()
    for copy in first + second + third:
        copy.wait_send()


def sum_all(n_row, n_col, name, collective_id, x):
    spec = pl.BlockSpec(memory_space=pltpu.VMEM)
    count = x.shape[0] // n_row
    dma = pltpu.SemaphoreType.DMA
    return pl.pallas_call(
        functools.partial(sum_kernel, n_row, n_col),
        out_shape=jax.ShapeDtypeStruct(x.shape, x.dtype),
        in_specs=[spec],
        out_specs=spec,
        scratch_shapes=[
            pltpu.VMEM((n_row, count, x.shape[1]), x.dtype),
            pltpu.VMEM((n_col, count, x.shape[1]), x.dtype),
            dma((n_row,)),
            dma((n_row,)),
            dma((n_col,)),
            dma((n_col,)),
            dma((n_row,)),
            dma((n_row,)),
        ],
        compiler_params=pltpu.CompilerParams(collective_id=collective_id, has_side_effects=True),
        cost_estimate=pl.CostEstimate(flops=10**9, bytes_accessed=10**7, transcendentals=0),
        name=name,
    )(x)


def place(n_row, n_col):
    return lax.axis_index("row") * n_col + lax.axis_index("col")


def greet_all(n_row, n_col):
    n = n_row * n_col
    me = place(n_row, n_col)
    barrier = pltpu.get_barrier_semaphore()

    def one(d, carry):
        peer = lax.rem(me + d, n)
        pl.semaphore_signal(
            barrier, inc=1, device_id=(peer // n_col, lax.rem(peer, n_col)), device_id_type=MESH
        )
        return carry

    lax.fori_loop(1, n, one, 0)
    pl.semaphore_wait(barrier, n - 1)


def exchange_copy(n_row, n_col, d, source, target, send, recv):
    n = n_row * n_col
    me = place(n_row, n_col)
    peer = lax.rem(me + d, n)
    return pltpu.make_async_remote_copy(
        src_ref=source.at[peer],
        dst_ref=target.at[me],
        send_sem=send.at[d],
        recv_sem=recv.at[d],
        device_id=(peer // n_col, lax.rem(peer, n_col)),
        device_id_type=MESH,
    )


def start_exchange(n_row, n_col, *refs):
    def one(d, carry):
        exchange_copy(n_row, n_col, d, *refs).start()
        return carry

    lax.fori_loop(1, n_row * n_col, one, 0)


def end_exchange(n_row, n_col, *refs):
    def one(d, carry):
        exchange_copy(n_row, n_col, d, *refs).wait()
        return carry

    lax.fori_loop(1, n_row * n_col, one, 0)


def front_kernel(
    n_row, n_col, flat_ref, three_ref, one_ref, two_ref,
    held_ref, turned_ref, all_one_ref, all_two_ref,
    parted, send, recv, s1, r1, s2, r2,
):
    row, col = lax.axis_index("row"), lax.axis_index("col")
    me = place(n_row, n_col)
    n, share, span = parted.shape
    contracted = cross_product(three_ref[...], flat_ref[...])
    for d in range(n):
        parted[d] = contracted[d * share : (d + 1) * share]
    greet_all(n_row, n_col)
    start_exchange(n_row, n_col, parted, held_ref, send, recv)
    count_one, count_two = one_ref.shape[0], two_ref.shape[0]
    own_one = pl.ds(pl.multiple_of(row * count_one, SUBLANES), count_one)
    own_two = pl.ds(pl.multiple_of(col * count_two, SUBLANES), count_two)
    made = []
    for d in range(1, n_row):
        made.append(
            pltpu.make_async_remote_copy(
                src_ref=one_ref,
                dst_ref=all_one_ref.at[own_one],
                send_sem=s1.at[d],
                recv_sem=r1.at[d],
                device_id=(lax.rem(row + d, n_row), col),
                device_id_type=MESH,
            )
        )
    for d in range(1, n_col):
        made.append(
            pltpu.make_async_remote_copy(
                src_ref=two_ref,
                dst_ref=all_two_ref.at[own_two],
                send_sem=s2.at[d],
                recv_sem=r2.at[d],
                device_id=(row, lax.rem(col + d, n_col)),
                device_id_type=MESH,
            )
        )
    for copy in made:
        copy.start()
    held_ref[me] = parted[me]
    all_one_ref[own_one, :] = one_ref[...]
    all_two_ref[own_two, :] = two_ref[...]
    turned_ref[...] = flat_ref[...].T
    for copy in made:
        copy.wait()
    end_exchange(n_row, n_col, parted, held_ref, send, recv)


def slab_kernel(n_row, n_col, send_ref, basis_ref, slab_ref, image_ref, send, recv):
    me = place(n_row, n_col)
    greet_all(n_row, n_col)
    start_exchange(n_row, n_col, send_ref, slab_ref, send, recv)
    slab_ref[me] = send_ref[me]
    end_exchange(n_row, n_col, send_ref, slab_ref, send, recv)
    n, cells, width = slab_ref.shape
    image_ref[...] = apply_gram(slab_ref[...].reshape(n * cells, width), basis_ref[...])


def linked(kernel, n_row, n_col, collective_id, shapes, scratch, *operands):
    outs = [jax.ShapeDtypeStruct(shape, jnp.float32) for shape in shapes]
    spec = pl.BlockSpec(memory_space=pltpu.VMEM)
    return pl.pallas_call(
        functools.partial(kernel, n_row, n_col),
        out_shape=outs,
        in_specs=[spec] * len(operands),
        out_specs=[spec] * len(outs),
        scratch_shapes=scratch,
        compiler_params=pltpu.CompilerParams(collective_id=collective_id, has_side_effects=True),
        cost_estimate=pl.CostEstimate(flops=10**9, bytes_accessed=10**7, transcendentals=0),
    )(*operands)


def shared(n_row, n_col, tensor, start_one, start_two, start_three):
    rows_one, rows_two, depth = tensor.shape
    rank = start_three.shape[1]
    both = ("row", "col")
    n = n_row * n_col
    n_one, n_two = rows_one * n_row, rows_two * n_col
    span, share, cells = rows_one * rows_two, rank // n, depth // n
    dma = pltpu.SemaphoreType.DMA

    held, turned, whole_one, whole_two = linked(
        front_kernel,
        n_row,
        n_col,
        3,
        [(n, share, span), (depth, span), (n_one, rank), (n_two, rank)],
        [
            pltpu.VMEM((n, share, span), jnp.float32),
            dma((n,)),
            dma((n,)),
            dma((n_row,)),
            dma((n_row,)),
            dma((n_col,)),
            dma((n_col,)),
        ],
        tensor.reshape(span, depth),
        start_three,
        start_one,
        start_two,
    )
    cube = lax.all_to_all(turned.reshape(n, cells, span), both, split_axis=0, concat_axis=0, tiled=True)
    held = held.reshape(n_row, n_col, share, rows_one, rows_two).transpose(2, 0, 3, 1, 4)
    held = held.reshape(share, n_one, n_two)

    add = functools.partial(sum_all, n_row, n_col)
    (part,) = on_core(gram_one_kernel, [(n_one, n_one)], held, whole_two)
    gram_one = add("sum_gram", 1, part)
    basis_one, part = on_core(
        mode_one_kernel, [(n_one, rank), (n_two, n_two)], gram_one, whole_one, held
    )
    gram_two = add("sum_gram", 1, part)
    own_a, own_b = rank // n_row, rank // n_col
    basis_two, blocks = on_core(
        functools.partial(mode_two_kernel, n_row, n_col),
        [(n_two, rank), (n, cells, own_a * own_b)],
        gram_two,
        whole_two,
        basis_one,
        cube,
        scratch=[(n_one * cells, n_two), (cells * rank, n_two)],
    )
    packed_shape = (depth // 2, 2 * rank)
    slab, part = linked(
        slab_kernel,
        n_row,
        n_col,
        4,
        [(n, cells, own_a * own_b), packed_shape],
        [dma((n,)), dma((n,))],
        blocks,
        start_three,
    )
    slab = slab.reshape(depth, own_a * own_b)
    for iteration in range(STEPS - 1):
        (part,) = on_core(image_kernel, [packed_shape], add("sum_image", 2, part), slab)
    factor_three, core = on_core(
        last_kernel,
        [(depth, rank), (rank, own_a * own_b)],
        add("sum_image", 2, part),
        slab,
    )
    factor_one = basis_one * math.sqrt(n_one)
    factor_two = basis_two * math.sqrt(n_two)
    return (factor_one, factor_two, factor_three, core.reshape(rank, own_a, own_b))


def solution(mesh):
    n_row, n_col = mesh.shape["row"], mesh.shape["col"]
    n = n_row * n_col

    def on_device(tensor, start_one, start_two, start_three):
        rows_one, rows_two, depth = tensor.shape
        rank = start_three.shape[1]
        even = (
            rank % n == 0
            and depth % (2 * n_row * SUBLANES) == 0
            and depth % (n * SUBLANES) == 0
            and rows_one % SUBLANES == 0
            and rows_one * n_row == rows_two * n_col == LANES
            and rank * rank == n * LANES
        )
        if even:
            return shared(n_row, n_col, tensor, start_one, start_two, start_three)
        return general(tensor, start_one, start_two, start_three)

    return jax.shard_map(
        on_device,
        mesh=mesh,
        in_specs=(P("row", "col", None), P("row", None), P("col", None), P()),
        out_specs=(P(), P(), P(), P(None, "row", "col")),
        check_vma=False,
    )
```

```python
import functools
import math

import jax
import jax.numpy as jnp
from jax import lax
from jax.experimental import pallas as pl
from jax.experimental.pallas import tpu as pltpu
from jax.sharding import PartitionSpec as P

STEPS = 4


HIGHEST = lax.Precision.HIGHEST
MESH = pl.DeviceIdType.MESH
SUBLANES = 8
LANES = 128


def product(left, right):
    return jnp.dot(left, right, precision=HIGHEST, preferred_element_type=jnp.float32)


def left_product(left, right):
    return lax.dot_general(
        left, right, (((0,), (0,)), ((), ())), precision=HIGHEST, preferred_element_type=jnp.float32
    )


def right_product(left, right):
    return lax.dot_general(
        left, right, (((1,), (1,)), ((), ())), precision=HIGHEST, preferred_element_type=jnp.float32
    )


def cross_product(left, right):
    return lax.dot_general(
        left, right, (((0,), (1,)), ((), ())), precision=HIGHEST, preferred_element_type=jnp.float32
    )


def orthonormal(matrix, inner):
    lower = jnp.linalg.cholesky(inner)
    return jax.scipy.linalg.solve_triangular(lower, matrix.T, lower=True).T


def settle(gram_whole, basis):
    for iteration in range(STEPS):
        image = product(gram_whole, basis)
        basis = orthonormal(image, left_product(image, image))
    return basis


def general(tensor, start_one, start_two, start_three):
    rows_one, rows_two, depth = tensor.shape
    rank = start_three.shape[1]
    flat = tensor.reshape(rows_one * rows_two, depth)
    contracted = cross_product(start_three, flat).reshape(rank, rows_one, rows_two)
    part_one = jnp.einsum("cij,jb->ibc", contracted, start_two, precision=HIGHEST).reshape(
        rows_one, rank * rank
    )
    slab_one = lax.psum_scatter(part_one, "col", scatter_dimension=1, tiled=True)
    slab_rows_one = lax.all_gather(slab_one, "row", axis=0, tiled=True)
    gram_one = lax.psum(right_product(slab_rows_one, slab_rows_one), "col")
    basis_one = settle(gram_one, lax.all_gather(start_one, "row", axis=0, tiled=True))
    own_one = lax.dynamic_slice_in_dim(basis_one, lax.axis_index("row") * rows_one, rows_one, 0)
    part_two = jnp.einsum("cij,ia->jac", contracted, own_one, precision=HIGHEST).reshape(
        rows_two, rank * rank
    )
    slab_two = lax.psum_scatter(part_two, "row", scatter_dimension=1, tiled=True)
    slab_rows_two = lax.all_gather(slab_two, "col", axis=0, tiled=True)
    gram_two = lax.psum(right_product(slab_rows_two, slab_rows_two), "row")
    basis_two = settle(gram_two, lax.all_gather(start_two, "col", axis=0, tiled=True))
    own_two = lax.dynamic_slice_in_dim(basis_two, lax.axis_index("col") * rows_two, rows_two, 0)
    received = lax.all_to_all(tensor, "row", split_axis=2, concat_axis=0, tiled=True)
    count, items, cells = received.shape
    merged = left_product(basis_one, received.reshape(count, items * cells))
    mixed = merged.reshape(rank, items, cells)
    part_three = jnp.einsum("ajk,jb->kba", mixed, own_two, precision=HIGHEST)
    cells_here = part_three.shape[0]
    slab_three = lax.psum_scatter(
        part_three.reshape(cells_here, rank * rank), "col", scatter_dimension=1, tiled=True
    )
    gram_part_three = right_product(slab_three, lax.all_gather(slab_three, "row", axis=0, tiled=True))
    gram_three = lax.psum(gram_part_three, "col")
    basis_three = start_three
    own_three = start_three
    for iteration in range(STEPS):
        image = product(gram_three, basis_three)
        inner = lax.psum(left_product(image, image), "row")
        own_three = orthonormal(image, inner)
        basis_three = lax.all_gather(own_three, "row", axis=0, tiled=True)
    core_part = left_product(own_three, slab_three)
    core_part = core_part.reshape(rank, core_part.shape[1] // rank, rank)
    core = lax.psum_scatter(core_part, "row", scatter_dimension=2, tiled=True).transpose(0, 2, 1)
    factor_one = basis_one * math.sqrt(basis_one.shape[0])
    factor_two = basis_two * math.sqrt(basis_two.shape[0])
    factor_three = basis_three * math.sqrt(basis_three.shape[0])
    return (factor_one, factor_two, factor_three, core)


def inverse_factor(inner):
    n = inner.shape[0]
    groups = n // SUBLANES
    eye = (
        lax.broadcasted_iota(jnp.int32, (n, n), 0) == lax.broadcasted_iota(jnp.int32, (n, n), 1)
    ).astype(jnp.float32)
    whole = jnp.concatenate([inner, eye], axis=1)
    width = whole.shape[1]
    rows = [whole[g * SUBLANES : (g + 1) * SUBLANES] for g in range(groups)]
    sub = lax.broadcasted_iota(jnp.int32, (SUBLANES, width), 0)
    pivots = [None] * n
    shape = (SUBLANES, width)
    for base in range(groups):
        columns = [
            [jnp.broadcast_to(rows[g][:, k : k + 1], shape) for g in range(base, groups)]
            for k in range(base * SUBLANES, (base + 1) * SUBLANES)
        ]
        for t in range(SUBLANES):
            pivot = jnp.broadcast_to(columns[t][0][t : t + 1, :], shape)
            scale = 1.0 / pivot
            pivots[base * SUBLANES + t] = pivot
            row = jnp.broadcast_to(rows[base][t : t + 1, :], shape)
            heads = [
                jnp.broadcast_to(columns[s][0][t : t + 1, :], shape) for s in range(t + 1, SUBLANES)
            ]
            for g in range(base, groups):
                factor = columns[t][g - base] * scale
                if g == base:
                    factor = jnp.where(sub > t, factor, 0.0)
                rows[g] = rows[g] - factor * row
                for s in range(t + 1, SUBLANES):
                    columns[s][g - base] = columns[s][g - base] - factor * heads[s - t - 1]
    out = []
    for g in range(groups):
        held = pivots[g * SUBLANES]
        for t in range(1, SUBLANES):
            held = jnp.where(sub == t, pivots[g * SUBLANES + t], held)
        out.append(rows[g] * lax.rsqrt(held))
    return jnp.concatenate(out, axis=0)[:, n:]


def orth(image):
    return right_product(image, inverse_factor(left_product(image, image)))


def steps_on(gram_ref, start_ref, basis_ref):
    basis_ref[...] = start_ref[...]

    def one(_, carry):
        basis_ref[...] = orth(product(gram_ref[...], basis_ref[...]))
        return carry

    lax.fori_loop(0, STEPS, one, 0)


def gram_one_kernel(held_ref, start_ref, gram_ref):
    slabs = [product(held_ref[c], start_ref[...]) for c in range(held_ref.shape[0])]
    total = right_product(slabs[0], slabs[0])
    for slab in slabs[1:]:
        total = total + right_product(slab, slab)
    gram_ref[...] = total


def mode_one_kernel(gram_ref, start_ref, held_ref, basis_ref, factor_ref, next_ref):
    steps_on(gram_ref, start_ref, basis_ref)
    basis = basis_ref[...]
    factor_ref[...] = (basis * math.sqrt(basis.shape[0])).T
    total = None
    for c in range(held_ref.shape[0]):
        slab = left_product(held_ref[c], basis)
        term = right_product(slab, slab)
        total = term if total is None else total + term
    next_ref[...] = total


def lane_groups(width):
    return lax.div(lax.broadcasted_iota(jnp.int32, (1, LANES), 1), width)


def shifted(value, amount):
    amount = amount % LANES
    return value if amount == 0 else pltpu.roll(value, amount, 1)


def mode_two_kernel(n_row, n_col, gram_ref, start_ref, one_ref, cube_ref, factor_ref, send_ref, basis_ref, cube, mixed):
    n, cells, span = cube_ref.shape
    width = LANES // n_col
    rows_one = span // width
    group = lane_groups(width)
    for row in range(n_row):
        for tile in range(span // LANES):
            blocks = [cube_ref[row * n_col + q, :, tile * LANES : (tile + 1) * LANES] for q in range(n_col)]
            for s in range(n_col):
                held = blocks[0]
                held = shifted(held, -s * width)
                for q in range(1, n_col):
                    held = jnp.where(group == q, shifted(blocks[q], (q - s) * width), held)
                item = row * rows_one + tile * n_col + s
                cube[item * cells : (item + 1) * cells, :] = held
    count, rank = one_ref.shape
    one = one_ref[...]
    for k in range(cells):
        face = cube[pl.ds(k, count, stride=cells), :]
        mixed[k * rank : (k + 1) * rank, :] = left_product(one, face)
    steps_on(gram_ref, start_ref, basis_ref)
    basis = basis_ref[...]
    factor_ref[...] = (basis * math.sqrt(basis.shape[0])).T
    wide = jnp.concatenate([basis, jnp.zeros((basis.shape[0], LANES - rank), jnp.float32)], axis=1)
    own_a, own_b = rank // n_row, rank // n_col
    group = lane_groups(own_b)
    for row in range(n_row):
        rows = [mixed[pl.ds(row * own_a + s, cells, stride=rank), :] for s in range(own_a)]
        slabs = product(jnp.concatenate(rows, axis=0), wide)
        for q in range(n_col):
            held = None
            for s in range(own_a):
                moved = shifted(slabs[s * cells : (s + 1) * cells], (s - q) * own_b)
                held = moved if held is None else jnp.where(group == s, moved, held)
            send_ref[row * n_col + q] = held


def pack(image):
    half = image.shape[0] // 2
    return jnp.concatenate([image[:half], image[half:]], axis=1)


def unpack(packed):
    half = packed.shape[1] // 2
    return jnp.concatenate([packed[:, :half], packed[:, half:]], axis=0)


def on_core(kernel, shapes, *operands, scratch=()):
    outs = [jax.ShapeDtypeStruct(shape, jnp.float32) for shape in shapes]
    spec = pl.BlockSpec(memory_space=pltpu.VMEM)
    cost = pl.CostEstimate(flops=2 * 10**9, bytes_accessed=2 * 10**6, transcendentals=0)
    return pl.pallas_call(
        kernel,
        out_shape=outs,
        in_specs=[spec] * len(operands),
        out_specs=[spec] * len(outs),
        scratch_shapes=[pltpu.VMEM(shape, jnp.float32) for shape in scratch],
        cost_estimate=cost,
    )(*operands)


def row_peer(n_row, d):
    return (lax.rem(lax.axis_index("row") + d, n_row), lax.axis_index("col"))


def col_peer(n_col, d):
    return (lax.axis_index("row"), lax.rem(lax.axis_index("col") + d, n_col))


def sum_body(n_row, n_col, x_ref, o_ref, parts, planes, s1, r1, s2, r2, s3, r3):
    row, col = lax.axis_index("row"), lax.axis_index("col")
    count = x_ref.shape[0] // n_row

    def mine(which):
        return pl.ds(pl.multiple_of(which * count, SUBLANES), count)

    def copies(n, peer, source, target, send, recv):
        made = [
            pltpu.make_async_remote_copy(
                src_ref=source(d),
                dst_ref=target(d),
                send_sem=send.at[d],
                recv_sem=recv.at[d],
                device_id=peer(n, d),
                device_id_type=MESH,
            )
            for d in range(1, n)
        ]
        for copy in made:
            copy.start()
        return made

    first = copies(
        n_row, row_peer, lambda d: x_ref.at[mine(row_peer(n_row, d)[0])], lambda d: parts.at[d], s1, r1
    )
    total = x_ref[mine(row), :]
    for d in range(1, n_row):
        first[d - 1].wait_recv()
        total = total + parts[d]
    planes[col] = total
    second = copies(n_col, col_peer, lambda d: planes.at[col], lambda d: planes.at[col], s2, r2)
    for copy in second:
        copy.wait_recv()
    total = planes[0]
    for q in range(1, n_col):
        total = total + planes[q]
    o_ref[mine(row), :] = total
    third = copies(n_row, row_peer, lambda d: o_ref.at[mine(row)], lambda d: o_ref.at[mine(row)], s3, r3)
    for copy in third:
        copy.wait_recv()
    for copy in first + second + third:
        copy.wait_send()


def sum_kernel(n_row, n_col, *refs):
    barrier = pltpu.get_barrier_semaphore()
    for d in range(1, n_row):
        pl.semaphore_signal(barrier, inc=1, device_id=row_peer(n_row, d), device_id_type=MESH)
    for d in range(1, n_col):
        pl.semaphore_signal(barrier, inc=1, device_id=col_peer(n_col, d), device_id_type=MESH)
    pl.semaphore_wait(barrier, n_row + n_col - 2)
    sum_body(n_row, n_col, *refs)


def sum_all(n_row, n_col, name, collective_id, x):
    spec = pl.BlockSpec(memory_space=pltpu.VMEM)
    count = x.shape[0] // n_row
    dma = pltpu.SemaphoreType.DMA
    return pl.pallas_call(
        functools.partial(sum_kernel, n_row, n_col),
        out_shape=jax.ShapeDtypeStruct(x.shape, x.dtype),
        in_specs=[spec],
        out_specs=spec,
        scratch_shapes=[
            pltpu.VMEM((n_row, count, x.shape[1]), x.dtype),
            pltpu.VMEM((n_col, count, x.shape[1]), x.dtype),
            dma((n_row,)),
            dma((n_row,)),
            dma((n_col,)),
            dma((n_col,)),
            dma((n_row,)),
            dma((n_row,)),
        ],
        compiler_params=pltpu.CompilerParams(collective_id=collective_id, has_side_effects=True),
        cost_estimate=pl.CostEstimate(flops=10**9, bytes_accessed=10**7, transcendentals=0),
        name=name,
    )(x)


def place(n_row, n_col):
    return lax.axis_index("row") * n_col + lax.axis_index("col")


def greet_all(n_row, n_col):
    n = n_row * n_col
    me = place(n_row, n_col)
    barrier = pltpu.get_barrier_semaphore()

    def one(d, carry):
        peer = lax.rem(me + d, n)
        pl.semaphore_signal(
            barrier, inc=1, device_id=(peer // n_col, lax.rem(peer, n_col)), device_id_type=MESH
        )
        return carry

    lax.fori_loop(1, n, one, 0)
    pl.semaphore_wait(barrier, n - 1)


def exchange_copy(n_row, n_col, d, source, target, send, recv):
    n = n_row * n_col
    me = place(n_row, n_col)
    peer = lax.rem(me + d, n)
    return pltpu.make_async_remote_copy(
        src_ref=source.at[peer],
        dst_ref=target.at[me],
        send_sem=send.at[d],
        recv_sem=recv.at[d],
        device_id=(peer // n_col, lax.rem(peer, n_col)),
        device_id_type=MESH,
    )


def start_exchange(n_row, n_col, *refs):
    def one(d, carry):
        exchange_copy(n_row, n_col, d, *refs).start()
        return carry

    lax.fori_loop(1, n_row * n_col, one, 0)


def end_exchange(n_row, n_col, *refs):
    def one(d, carry):
        exchange_copy(n_row, n_col, d, *refs).wait()
        return carry

    lax.fori_loop(1, n_row * n_col, one, 0)


def front_kernel(
    n_row, n_col, flat_ref, three_ref, one_ref, two_ref,
    held_ref, turned_ref, all_one_ref, all_two_ref,
    parted, send, recv, s1, r1, s2, r2,
):
    row, col = lax.axis_index("row"), lax.axis_index("col")
    me = place(n_row, n_col)
    n, share, span = parted.shape
    contracted = right_product(three_ref[...], flat_ref[...])
    for d in range(n):
        parted[d] = contracted[d * share : (d + 1) * share]
    greet_all(n_row, n_col)
    start_exchange(n_row, n_col, parted, held_ref, send, recv)
    count_one, count_two = one_ref.shape[0], two_ref.shape[0]
    own_one = pl.ds(pl.multiple_of(row * count_one, SUBLANES), count_one)
    own_two = pl.ds(pl.multiple_of(col * count_two, SUBLANES), count_two)
    made = []
    for d in range(1, n_row):
        made.append(
            pltpu.make_async_remote_copy(
                src_ref=one_ref,
                dst_ref=all_one_ref.at[own_one],
                send_sem=s1.at[d],
                recv_sem=r1.at[d],
                device_id=(lax.rem(row + d, n_row), col),
                device_id_type=MESH,
            )
        )
    for d in range(1, n_col):
        made.append(
            pltpu.make_async_remote_copy(
                src_ref=two_ref,
                dst_ref=all_two_ref.at[own_two],
                send_sem=s2.at[d],
                recv_sem=r2.at[d],
                device_id=(row, lax.rem(col + d, n_col)),
                device_id_type=MESH,
            )
        )
    for copy in made:
        copy.start()
    held_ref[me] = parted[me]
    all_one_ref[own_one, :] = one_ref[...]
    all_two_ref[own_two, :] = two_ref[...]
    turned_ref[...] = flat_ref[...].T
    for copy in made:
        copy.wait()
    end_exchange(n_row, n_col, parted, held_ref, send, recv)


def tail_kernel(
    n_row, n_col, send_ref, start_ref, factor_ref, core_ref,
    slab_ref, image, summed, parts, planes, send, recv, s1, r1, s2, r2, s3, r3,
):
    me = place(n_row, n_col)
    greet_all(n_row, n_col)
    start_exchange(n_row, n_col, send_ref, slab_ref, send, recv)
    slab_ref[me] = send_ref[me]
    end_exchange(n_row, n_col, send_ref, slab_ref, send, recv)
    n, cells, width = slab_ref.shape

    def slab():
        return slab_ref[...].reshape(n * cells, width)

    image[...] = pack(product(slab(), cross_product(slab(), start_ref[...])))

    def one(step, carry):
        turn = lax.rem(step, 2)
        sum_body(
            n_row, n_col, image, summed, parts, planes.at[turn],
            s1, r1, s2.at[turn], r2.at[turn], s3, r3,
        )
        now = unpack(summed[...])
        inverse = inverse_factor(left_product(now, now))

        @pl.when(step < STEPS - 1)
        def _():
            basis = right_product(now, inverse)
            image[...] = pack(product(slab(), left_product(slab(), basis)))

        @pl.when(step == STEPS - 1)
        def _():
            turned = right_product(inverse, now)
            factor_ref[...] = turned * math.sqrt(turned.shape[1])
            core_ref[...] = cross_product(slab(), turned)

        return carry

    lax.fori_loop(0, STEPS, one, 0)


def linked(kernel, n_row, n_col, collective_id, shapes, scratch, *operands):
    outs = [jax.ShapeDtypeStruct(shape, jnp.float32) for shape in shapes]
    spec = pl.BlockSpec(memory_space=pltpu.VMEM)
    return pl.pallas_call(
        functools.partial(kernel, n_row, n_col),
        out_shape=outs,
        in_specs=[spec] * len(operands),
        out_specs=[spec] * len(outs),
        scratch_shapes=scratch,
        compiler_params=pltpu.CompilerParams(collective_id=collective_id, has_side_effects=True),
        cost_estimate=pl.CostEstimate(flops=10**9, bytes_accessed=10**7, transcendentals=0),
    )(*operands)


def shared(n_row, n_col, tensor, start_one, start_two, start_three):
    rows_one, rows_two, depth = tensor.shape
    rank = start_three.shape[1]
    both = ("row", "col")
    n = n_row * n_col
    n_one, n_two = rows_one * n_row, rows_two * n_col
    span, share, cells = rows_one * rows_two, rank // n, depth // n
    dma = pltpu.SemaphoreType.DMA

    held, turned, whole_one, whole_two = linked(
        front_kernel,
        n_row,
        n_col,
        3,
        [(n, share, span), (depth, span), (n_one, rank), (n_two, rank)],
        [
            pltpu.VMEM((n, share, span), jnp.float32),
            dma((n,)),
            dma((n,)),
            dma((n_row,)),
            dma((n_row,)),
            dma((n_col,)),
            dma((n_col,)),
        ],
        tensor.reshape(span, depth),
        start_three.T,
        start_one,
        start_two,
    )
    cube = lax.all_to_all(turned.reshape(n, cells, span), both, split_axis=0, concat_axis=0, tiled=True)
    held = held.reshape(n_row, n_col, share, rows_one, rows_two).transpose(2, 0, 3, 1, 4)
    held = held.reshape(share, n_one, n_two)

    add = functools.partial(sum_all, n_row, n_col)
    (part,) = on_core(gram_one_kernel, [(n_one, n_one)], held, whole_two)
    gram_one = add("sum_gram", 1, part)
    basis_one, factor_one, part = on_core(
        mode_one_kernel, [(n_one, rank), (rank, n_one), (n_two, n_two)], gram_one, whole_one, held
    )
    gram_two = add("sum_gram", 1, part)
    own_a, own_b = rank // n_row, rank // n_col
    factor_two, blocks = on_core(
        functools.partial(mode_two_kernel, n_row, n_col),
        [(rank, n_two), (n, cells, own_a * own_b)],
        gram_two,
        whole_two,
        basis_one,
        cube,
        scratch=[(n_two, rank), (n_one * cells, n_two), (cells * rank, n_two)],
    )
    packed, count = (depth // 2, 2 * rank), depth // 2 // n_row
    factor_three, core = linked(
        tail_kernel,
        n_row,
        n_col,
        4,
        [(rank, depth), (own_a * own_b, rank)],
        [
            pltpu.VMEM((n, cells, own_a * own_b), jnp.float32),
            pltpu.VMEM(packed, jnp.float32),
            pltpu.VMEM(packed, jnp.float32),
            pltpu.VMEM((n_row, count, 2 * rank), jnp.float32),
            pltpu.VMEM((2, n_col, count, 2 * rank), jnp.float32),
            dma((n,)),
            dma((n,)),
            dma((n_row,)),
            dma((n_row,)),
            dma((2, n_col)),
            dma((2, n_col)),
            dma((n_row,)),
            dma((n_row,)),
        ],
        blocks,
        start_three.T,
    )
    factor_three = factor_three.T
    return (factor_one.T, factor_two.T, factor_three, core.reshape(own_a, own_b, rank).transpose(2, 0, 1))


def solution(mesh):
    n_row, n_col = mesh.shape["row"], mesh.shape["col"]
    n = n_row * n_col

    def on_device(tensor, start_one, start_two, start_three):
        rows_one, rows_two, depth = tensor.shape
        rank = start_three.shape[1]
        even = (
            rank % n == 0
            and depth % (2 * n_row * SUBLANES) == 0
            and depth % (n * SUBLANES) == 0
            and rows_one % SUBLANES == 0
            and rows_one * n_row == rows_two * n_col == LANES
            and rank * rank == n * LANES
        )
        if even:
            return shared(n_row, n_col, tensor, start_one, start_two, start_three)
        return general(tensor, start_one, start_two, start_three)

    return jax.shard_map(
        on_device,
        mesh=mesh,
        in_specs=(P("row", "col", None), P("row", None), P("col", None), P()),
        out_specs=(P(), P(), P(), P(None, "row", "col")),
        check_vma=False,
    )
```
